512 devices in a mesh: grp: 16 (over y, core), ops: 32 (over x, z).
Axes of the slice: x: 4, y: 8, z: 8, core: 2. Of those that a mesh axis runs over, the one named last changes fastest.
Arguments:
- op_embed: bfloat16 [131072, 256], P(('grp', 'ops')), may hold values from -6 to 6
- machine_embed: bfloat16 [8192, 256], P('grp'), may hold values from -6 to 6
- cotangent: bfloat16 [131072, 256], P(('grp', 'ops')), may hold values from -6 to 6
- w_query: bfloat16 [256, 256], replicated, may hold values from -0.375 to 0.375
- w_key: bfloat16 [256, 256], replicated, may hold values from -0.375 to 0.375
- w_value: bfloat16 [256, 256], replicated, may hold values from -0.375 to 0.375
- slot_local: int32 [512, 16], P(('grp', 'ops')), may hold values from 0 to 3
- counts: int32 [131072, 16], P(('grp', 'ops')), may hold values from 0 to 128, as said below
Outputs:
- op_grad: bfloat16 [131072, 256], P(('grp', 'ops'))
- machine_grad: float32 [8192, 256], P(('grp', 'ops'))
- grad_wq: float32 [256, 256], replicated
- grad_wk: float32 [256, 256], replicated
- grad_wv: float32 [256, 256], replicated
The draws below stay inside these ranges and needn't reach their ends.
Inputs may be any that keep to these rules, and one draw needn't show every extreme that they name: The eligible machines of slot e's block for operation o are its first counts[o, e] machines; 0 means the operation has no eligible machine in that block.
All inputs are finite; a program needn't handle non-finite values.
Results may differ from the reference program's by a relative error of at most 0.0056.
Values may be sent and summed in bfloat16 or wider, within the bound.
No kernel may reach another device: no remote copies, remote signals or barrier semaphores. Data moves between devices by JAX's collectives and lax.ppermute only.
A program may use at most 64 MiB of HBM per device.

```python
import jax
import jax.numpy as jnp
from jax import lax

D = 256
HEADS = 8
BLK = 128
OPS_DEV = 256
MBLK = 4
SHARDS = 512
NOPS = 131072
NMACH = 8192
N_GRP = 16


def draw_counts(key, part):
    first_key, second_key, third_key = jax.random.split(key, 3)
    tiles_dev = OPS_DEV // BLK
    lengths = jax.random.randint(first_key, (NOPS, N_GRP), 1, BLK + 1)
    levels = jax.random.randint(second_key, (SHARDS,), 1, 8)
    chances = jax.random.randint(third_key, (SHARDS, tiles_dev, N_GRP), 0, 8)
    live_tiles = chances < levels[:, None, None]
    live_rows = jnp.repeat(live_tiles, BLK, axis=1).reshape(NOPS, N_GRP)
    result = jnp.where(live_rows, lengths, 0)
    result = result.at[0, 0].set(BLK)
    result = result.at[NOPS - 1, N_GRP - 1].set(0)
    return result.astype(jnp.int32)


def touch_ends(values, key, low, largest):
    index_at = [jax.random.randint(jax.random.fold_in(key, axis), (), 0, length) for axis, length in enumerate(values.shape)]
    main_axis = values.shape.index(max(values.shape))
    beside = index_at[:main_axis] + [(index_at[main_axis] + 1) % values.shape[main_axis]] + index_at[main_axis + 1:]
    return values.at[tuple(index_at)].set(low).at[tuple(beside)].set(largest)


def shard_levels(key, dims, shards, least, high):
    def one(axis_at, blocks):
        steps = jax.random.uniform(jax.random.fold_in(jax.random.fold_in(key, 6), axis_at), (blocks,), jnp.float32, least / len(shards), high / len(shards))
        return jnp.repeat(jnp.exp(steps), dims[axis_at] // blocks).reshape((-1,) + (1,) * (len(dims) - axis_at - 1))

    gain = one(*shards[0])
    for cut in shards[1:]:
        gain = gain * one(*cut)
    return gain


def noise(stream_key, shape, spread, bound, cuts=(), kind=jnp.bfloat16):
    values = jax.random.normal(stream_key, shape, jnp.float32) * spread
    if len(cuts) > 0:
        values = shard_levels(stream_key, shape, cuts, -0.22, 0.18) * values
    return jnp.clip(values, min=-bound, max=bound).astype(kind)


def setup_inputs(seed: int = 0) -> dict:
    streams_of = jax.random.split(jax.random.key(seed), 9)
    return {
        "op_embed": noise(streams_of[0], (NOPS, D), 1.0, 6.0, ((0, 512),)),
        "machine_embed": noise(streams_of[1], (NMACH, D), 1.0, 6.0, ((0, 16),)),
        "cotangent": noise(streams_of[2], (NOPS, D), 1.0, 6.0, ((0, 512),)),
        "w_query": noise(streams_of[3], (D, D), D ** -0.5, 0.375),
        "w_key": noise(streams_of[4], (D, D), D ** -0.5, 0.375),
        "w_value": noise(streams_of[5], (D, D), D ** -0.5, 0.375),
        "slot_local": touch_ends(jax.random.randint(streams_of[6], (SHARDS, N_GRP), 0, MBLK), jax.random.fold_in(streams_of[6], 1), 0, MBLK - 1).astype(jnp.int32),
        "counts": draw_counts(jax.random.fold_in(streams_of[8], 71), 0),
    }


mean_scale = 0.08838834764831845


def slot_terms(queries, cotangent4, key_rows, value_rows, lengths):
    head_size = queries.shape[2]
    inv_root = head_size ** -0.5
    query_f = queries.astype(jnp.float32)
    cot_f = cotangent4.astype(jnp.float32)
    key_f = key_rows.astype(jnp.float32)
    value_f = value_rows.astype(jnp.float32)
    scores = jnp.einsum('ohc,mhc->ohm', query_f, key_f) * inv_root
    sigmoid_score = jax.nn.sigmoid(scores)
    columns = lax.broadcasted_iota(jnp.int32, scores.shape, 2)
    eligible = columns < lengths[:, None, None]
    gates = jnp.where(eligible, sigmoid_score, 0.0).astype(jnp.bfloat16)
    value_dot = jnp.einsum('ohc,mhc->ohm', cot_f, value_f)
    dscore = jnp.where(eligible, mean_scale * value_dot * sigmoid_score * (1.0 - sigmoid_score) * inv_root, 0.0).astype(jnp.bfloat16)
    dscore_f = dscore.astype(jnp.float32)
    query_part = jnp.einsum('ohm,mhc->ohc', dscore_f, key_f)
    key_grad = jnp.einsum('ohm,ohc->mhc', dscore_f, query_f).astype(jnp.bfloat16)
    value_grad = (mean_scale * jnp.einsum('ohm,ohc->mhc', gates.astype(jnp.float32), cot_f)).astype(jnp.bfloat16)
    return query_part, key_grad, value_grad


def reference(op_embed, machine_embed, cotangent, w_query, w_key, w_value, slot_local, counts):
    model_width = op_embed.shape[1]
    head_size = model_width // HEADS
    highest = lax.Precision.HIGHEST
    queries = jnp.dot(op_embed, w_query, preferred_element_type=jnp.float32).astype(jnp.bfloat16)
    key_rows = jnp.dot(machine_embed, w_key, preferred_element_type=jnp.float32).astype(jnp.bfloat16)
    value_rows = jnp.dot(machine_embed, w_value, preferred_element_type=jnp.float32).astype(jnp.bfloat16)
    key_blocks = key_rows.reshape(N_GRP * MBLK, BLK, HEADS, head_size)
    value_blocks = value_rows.reshape(N_GRP * MBLK, BLK, HEADS, head_size)
    query_dev = queries.reshape(SHARDS, OPS_DEV, HEADS, head_size)
    cot_dev = cotangent.reshape(SHARDS, OPS_DEV, HEADS, head_size)
    count_dev = counts.reshape(SHARDS, OPS_DEV, N_GRP)
    block_ids = (jnp.arange(N_GRP, dtype=jnp.int32)[None, :] * MBLK + slot_local).astype(jnp.int32)

    def per_device(carry, pieces):
        query_here, cot_here, count_here, ids_here = pieces

        def per_slot(inner, slot_index):
            summed_q, sum_keys, sum_values = inner
            block_id = ids_here[slot_index]
            query_part, key_grad, value_grad = slot_terms(query_here, cot_here, key_blocks[block_id], value_blocks[block_id], count_here[:, slot_index])
            sum_keys = sum_keys.at[block_id].add(key_grad.astype(jnp.float32))
            sum_values = sum_values.at[block_id].add(value_grad.astype(jnp.float32))
            return (summed_q + query_part, sum_keys, sum_values), None

        start_q = jnp.zeros((OPS_DEV, HEADS, head_size), jnp.float32)
        (summed_q, sum_keys, sum_values), _ = lax.scan(per_slot, (start_q, carry[0], carry[1]), jnp.arange(N_GRP, dtype=jnp.int32))
        return (sum_keys, sum_values), summed_q.astype(jnp.bfloat16)

    zero_blocks = jnp.zeros((N_GRP * MBLK, BLK, HEADS, head_size), jnp.float32)
    (sum_keys, sum_values), grad_rows = lax.scan(per_device, (zero_blocks, zero_blocks), (query_dev, cot_dev, count_dev, block_ids))
    grad_query = grad_rows.reshape(NOPS, model_width)
    op_grad = (cotangent.astype(jnp.float32) + jnp.dot(grad_query, w_query.T, preferred_element_type=jnp.float32)).astype(jnp.bfloat16)
    key_total = sum_keys.reshape(NMACH, model_width)
    value_total = sum_values.reshape(NMACH, model_width)
    machine_grad = jnp.dot(key_total, w_key.astype(jnp.float32).T, precision=highest) + jnp.dot(value_total, w_value.astype(jnp.float32).T, precision=highest)
    embed_f = machine_embed.astype(jnp.float32)
    grad_wq = jnp.dot(op_embed.T, grad_query, preferred_element_type=jnp.float32) / SHARDS
    grad_wk = jnp.dot(embed_f.T, key_total, precision=highest) / SHARDS
    grad_wv = jnp.dot(embed_f.T, value_total, precision=highest) / SHARDS
    return (op_grad, machine_grad, grad_wq, grad_wk, grad_wv)
```

```python
import functools

import jax
import jax.numpy as jnp
from jax import lax
from jax.experimental import pallas as pl
from jax.experimental.pallas import tpu as pltpu
from jax.sharding import PartitionSpec as P

HEADS = 8
BLK = 128
MEAN_SCALE = 0.08838834764831845

f32 = jnp.float32
bf16 = jnp.bfloat16
VMEM_SPEC = pl.BlockSpec(memory_space=pltpu.VMEM)
SMEM_SPEC = pl.BlockSpec(memory_space=pltpu.SMEM)


def dot(a, b):
    return jnp.dot(a, b, preferred_element_type=f32)


def dot_nt(a, b):
    return lax.dot_general(a, b, (((1,), (1,)), ((), ())), preferred_element_type=f32)


def dot_tn(a, b):
    return lax.dot_general(a, b, (((0,), (0,)), ((), ())), preferred_element_type=f32)


def attend_kernel(
    rows_ref,
    counts_ref,
    op_ref,
    cot_ref,
    wq_ref,
    wk_ref,
    wv_ref,
    wkt_ref,
    back_ref,
    opg_ref,
    wgrad_ref,
    qm_ref,
    cm_ref,
    gq_ref,
):
    step = pl.program_id(0)
    slots, blk, width = rows_ref.shape
    ops_count = op_ref.shape[0]
    head_size = width // HEADS
    inv_root = head_size ** (-0.5)
    machines = slots * blk

    @pl.when(step == 0)
    def _():
        queries = dot(op_ref[...], wq_ref[...]).astype(bf16)
        cot = cot_ref[...]
        lane_head = lax.broadcasted_iota(jnp.int32, (ops_count, width), 1) // head_size
        zero = jnp.zeros((), bf16)
        for h in range(HEADS):
            here = lane_head == h
            qm_ref[pl.ds(h * ops_count, ops_count), :] = jnp.where(here, queries, zero)
            cm_ref[pl.ds(h * ops_count, ops_count), :] = jnp.where(here, cot, zero)
        gq_ref[...] = jnp.zeros_like(gq_ref)
        wgrad_ref[pl.ds(width, 2 * width), :] = jnp.zeros((2 * width, width), f32)

    embed = rows_ref[...].reshape(machines, width)
    keys = dot(embed, wk_ref[...]).astype(bf16)
    values = dot(embed, wv_ref[...]).astype(bf16)
    keys_t = dot_nt(wkt_ref[...], embed).astype(bf16)
    place = lax.broadcasted_iota(jnp.int32, (blk, ops_count), 0)
    eligible = jnp.concatenate(
        [place < counts_ref[s, 0:1, :] for s in range(slots)], axis=0
    )
    key_grad = jnp.zeros((machines, width), f32)
    value_grad = jnp.zeros((machines, width), f32)
    for h in range(HEADS):
        q_h = qm_ref[pl.ds(h * ops_count, ops_count), :]
        c_h = cm_ref[pl.ds(h * ops_count, ops_count), :]
        scores = dot_nt(keys, q_h)
        value_dot = dot_nt(values, c_h)
        half = jnp.tanh(scores * (0.5 * inv_root))
        gate2 = jnp.where(eligible, 1.0 + half, 0.0).astype(bf16)
        slope = jnp.where(eligible, value_dot * (1.0 - half * half), 0.0).astype(bf16)
        key_grad += dot(slope, q_h)
        value_grad += dot(gate2, c_h)
        gq_ref[pl.ds(h * head_size, head_size), :] += dot(
            keys_t[h * head_size : (h + 1) * head_size, :], slope
        )
    d_scale = 0.25 * MEAN_SCALE * inv_root
    key_grad = (key_grad * d_scale).astype(bf16)
    value_grad = (value_grad * (0.5 * MEAN_SCALE)).astype(bf16)
    back = dot_nt(key_grad, wk_ref[...]) + dot_nt(value_grad, wv_ref[...])
    back_ref[...] = back.reshape(slots, blk, width).astype(bf16)
    wgrad_ref[pl.ds(width, width), :] += dot_tn(embed, key_grad)
    wgrad_ref[pl.ds(2 * width, width), :] += dot_tn(embed, value_grad)

    @pl.when(step == pl.num_programs(0) - 1)
    def _():
        grad_query = (gq_ref[...] * d_scale).T.astype(bf16)
        opg_ref[...] = (
            cot_ref[...].astype(f32) + dot_nt(grad_query, wq_ref[...])
        ).astype(bf16)
        wgrad_ref[pl.ds(0, width), :] = dot_tn(op_ref[...], grad_query)


def attend(rows, counts_t, op_embed, cotangent, w_query, w_key, w_value):
    slots, blk, width = rows.shape
    ops_count = op_embed.shape[0]
    pair = 2
    full = lambda shape: pl.BlockSpec(shape, lambda i: (0,) * len(shape))
    steps = slots // pair
    weight = full((width, width))
    return pl.pallas_call(
        attend_kernel,
        grid=(steps,),
        in_specs=[
            pl.BlockSpec((pair, blk, width), lambda i: (i, 0, 0)),
            pl.BlockSpec((pair, 1, ops_count), lambda i: (i, 0, 0)),
            full((ops_count, width)),
            full((ops_count, width)),
            weight,
            weight,
            weight,
            weight,
        ],
        out_specs=[
            pl.BlockSpec((pair, blk, width), lambda i: (i, 0, 0)),
            full((ops_count, width)),
            full((3 * width, width)),
        ],
        out_shape=[
            jax.ShapeDtypeStruct((slots, blk, width), bf16),
            jax.ShapeDtypeStruct((ops_count, width), bf16),
            jax.ShapeDtypeStruct((3 * width, width), f32),
        ],
        scratch_shapes=[
            pltpu.VMEM((HEADS * ops_count, width), bf16),
            pltpu.VMEM((HEADS * ops_count, width), bf16),
            pltpu.VMEM((width, ops_count), f32),
        ],
        compiler_params=pltpu.CompilerParams(dimension_semantics=("arbitrary",)),
        name="attend",
    )(
        rows,
        counts_t.reshape(slots, 1, ops_count),
        op_embed,
        cotangent,
        w_query,
        w_key,
        w_value,
        w_key.T,
    )


def pick_kernel(ids_ref, blocks_ref, out_ref):
    for g in range(out_ref.shape[0]):
        out_ref[g] = blocks_ref[ids_ref[g]]


def pick_blocks(ids, blocks):
    return pl.pallas_call(
        pick_kernel,
        in_specs=[SMEM_SPEC, VMEM_SPEC],
        out_specs=VMEM_SPEC,
        out_shape=jax.ShapeDtypeStruct((ids.shape[0],) + blocks.shape[1:], blocks.dtype),
        name="pick_blocks",
    )(ids, blocks)


def collect_kernel(ids_ref, parts_ref, out_ref, acc_ref):
    acc_ref[...] = jnp.zeros_like(acc_ref)
    for g in range(parts_ref.shape[0]):
        acc_ref[ids_ref[g]] += parts_ref[g].astype(f32)
    out_ref[...] = acc_ref[...].astype(out_ref.dtype)


def collect_blocks(ids, parts, blocks):
    shape = (blocks,) + parts.shape[1:]
    return pl.pallas_call(
        collect_kernel,
        in_specs=[SMEM_SPEC, VMEM_SPEC],
        out_specs=VMEM_SPEC,
        out_shape=jax.ShapeDtypeStruct(shape, bf16),
        scratch_shapes=[pltpu.VMEM(shape, f32)],
        name="collect_blocks",
    )(ids, parts)


def swap(x, axis):
    return lax.all_to_all(x, axis, split_axis=0, concat_axis=0, tiled=True)


def per_device(op_embed, machine_embed, cotangent, w_query, w_key, w_value, slot_local, counts):
    groups = lax.axis_size("grp")
    shards = lax.axis_size("ops")
    width = op_embed.shape[1]
    machine_rows = machine_embed.shape[0]
    blocks_here = machine_rows // BLK
    ids = swap(slot_local.reshape(groups, 1), "grp")[:, 0]
    outgoing = pick_blocks(ids, machine_embed.reshape(blocks_here, BLK, width))
    rows = swap(outgoing, "grp")
    back, op_grad, wgrad = attend(
        rows, counts.T, op_embed, cotangent, w_query, w_key, w_value
    )
    returned = swap(back, "grp")
    group_sum = collect_blocks(ids, returned, blocks_here)
    shares = swap(group_sum.reshape(shards, machine_rows // shards, width), "ops")
    machine_grad = jnp.sum(shares.astype(f32), axis=0)

    lead = 3 * width // shards
    scattered = swap(wgrad.astype(bf16).reshape(shards, lead, width), "ops")
    part = jnp.sum(scattered.astype(f32), axis=0).astype(bf16)
    crossed = swap(jnp.broadcast_to(part[None], (groups, lead, width)), "grp")
    mean = jnp.sum(crossed.astype(f32), axis=0) * (1.0 / (groups * shards))
    spread = swap(
        jnp.broadcast_to(mean.astype(bf16)[None], (shards, lead, width)), "ops"
    )
    total = spread.astype(f32).reshape(3, width, width)
    return (op_grad, machine_grad, total[0], total[1], total[2])


def solution(mesh):
    return jax.shard_map(
        per_device,
        mesh=mesh,
        in_specs=(
            P(("grp", "ops"), None),
            P("grp", None),
            P(("grp", "ops"), None),
            P(),
            P(),
            P(),
            P(("grp", "ops"), None),
            P(("grp", "ops"), None),
        ),
        out_specs=(P(("grp", "ops"), None), P(("grp", "ops"), None), P(), P(), P()),
        check_vma=False,
    )
```

```python
import functools

import jax
import jax.numpy as jnp
from jax import lax
from jax.experimental import pallas as pl
from jax.experimental.pallas import tpu as pltpu
from jax.sharding import PartitionSpec as P

HEADS = 8
BLK = 128
MEAN_SCALE = 0.08838834764831845

f32 = jnp.float32
bf16 = jnp.bfloat16
VMEM_SPEC = pl.BlockSpec(memory_space=pltpu.VMEM)
SMEM_SPEC = pl.BlockSpec(memory_space=pltpu.SMEM)


def dot(a, b):
    return jnp.dot(a, b, preferred_element_type=f32)


def dot_nt(a, b):
    return lax.dot_general(a, b, (((1,), (1,)), ((), ())), preferred_element_type=f32)


def dot_tn(a, b):
    return lax.dot_general(a, b, (((0,), (0,)), ((), ())), preferred_element_type=f32)


def attend_kernel(
    rows_ref,
    counts_ref,
    op_ref,
    cot_ref,
    wq_ref,
    wk_ref,
    wv_ref,
    wkt_ref,
    back_ref,
    opg_ref,
    wgrad_ref,
    qm_ref,
    cm_ref,
    gq_ref,
    wkv_ref,
):
    slots, blk, width = rows_ref.shape
    ops_count = op_ref.shape[0]
    head_size = width // HEADS
    inv_root = head_size ** (-0.5)
    d_scale = 0.25 * MEAN_SCALE * inv_root
    pair = 2
    machines = pair * blk

    queries = dot(op_ref[...], wq_ref[...]).astype(bf16)
    cot = cot_ref[...]
    lane_head = lax.broadcasted_iota(jnp.int32, (ops_count, width), 1) // head_size
    zero = jnp.zeros((), bf16)
    for h in range(HEADS):
        here = lane_head == h
        qm_ref[pl.ds(h * ops_count, ops_count), :] = jnp.where(here, queries, zero)
        cm_ref[pl.ds(h * ops_count, ops_count), :] = jnp.where(here, cot, zero)
    gq_ref[...] = jnp.zeros_like(gq_ref)
    wkv_ref[...] = jnp.zeros_like(wkv_ref)

    def one_pair(step, carry):
        first = step * pair
        embed = rows_ref[pl.ds(first, pair)].reshape(machines, width)
        keys = dot(embed, wk_ref[...]).astype(bf16)
        values = dot(embed, wv_ref[...]).astype(bf16)
        keys_t = dot_nt(wkt_ref[...], embed).astype(bf16)
        place = lax.broadcasted_iota(jnp.int32, (blk, ops_count), 0)
        eligible = jnp.concatenate(
            [place < counts_ref[first + s] for s in range(pair)], axis=0
        )
        key_grad = jnp.zeros((machines, width), f32)
        value_grad = jnp.zeros((machines, width), f32)
        for h in range(HEADS):
            q_h = qm_ref[pl.ds(h * ops_count, ops_count), :]
            c_h = cm_ref[pl.ds(h * ops_count, ops_count), :]
            scores = dot_nt(keys, q_h)
            value_dot = dot_nt(values, c_h)
            half = jnp.tanh(scores * (0.5 * inv_root))
            gate2 = jnp.where(eligible, 1.0 + half, 0.0).astype(bf16)
            slope = jnp.where(eligible, value_dot * (1.0 - half * half), 0.0).astype(bf16)
            key_grad += dot(slope, q_h)
            value_grad += dot(gate2, c_h)
            gq_ref[pl.ds(h * head_size, head_size), :] += dot(
                keys_t[h * head_size : (h + 1) * head_size, :], slope
            )
        key_grad = (key_grad * d_scale).astype(bf16)
        value_grad = (value_grad * (0.5 * MEAN_SCALE)).astype(bf16)
        back = dot_nt(key_grad, wk_ref[...]) + dot_nt(value_grad, wv_ref[...])
        back = back.astype(bf16)
        for s in range(pair):
            back_ref[first + s, 0:blk, :] = back[s * blk : (s + 1) * blk]
        wkv_ref[0:width, :] += dot_tn(embed, key_grad)
        wkv_ref[width : 2 * width, :] += dot_tn(embed, value_grad)
        return carry

    lax.fori_loop(0, slots // pair, one_pair, 0)
    grad_query = (gq_ref[...] * d_scale).T.astype(bf16)
    opg_ref[...] = (cot.astype(f32) + dot_nt(grad_query, wq_ref[...])).astype(bf16)
    wgrad_ref[0:width, :] = dot_tn(op_ref[...], grad_query).astype(bf16)
    wgrad_ref[width : 3 * width, :] = wkv_ref[...].astype(bf16)


def attend(rows, counts_t, op_embed, cotangent, w_query, w_key, w_value, extra=0):
    slots, blk, width = rows.shape
    ops_count = op_embed.shape[0]
    return pl.pallas_call(
        attend_kernel,
        in_specs=[VMEM_SPEC] * 8,
        out_specs=[VMEM_SPEC] * 3,
        out_shape=[
            jax.ShapeDtypeStruct((slots, blk + extra, width), bf16),
            jax.ShapeDtypeStruct((ops_count, width), bf16),
            jax.ShapeDtypeStruct((3 * width, width), bf16),
        ],
        scratch_shapes=[
            pltpu.VMEM((HEADS * ops_count, width), bf16),
            pltpu.VMEM((HEADS * ops_count, width), bf16),
            pltpu.VMEM((width, ops_count), f32),
            pltpu.VMEM((2 * width, width), f32),
        ],
        name="attend",
    )(
        rows,
        counts_t.reshape(slots, 1, ops_count),
        op_embed,
        cotangent,
        w_query,
        w_key,
        w_value,
        w_key.T,
    )


def pick_kernel(ids_ref, blocks_ref, out_ref):
    for g in range(out_ref.shape[0]):
        out_ref[g] = blocks_ref[ids_ref[g]]


def pick_blocks(ids, blocks):
    return pl.pallas_call(
        pick_kernel,
        in_specs=[SMEM_SPEC, VMEM_SPEC],
        out_specs=VMEM_SPEC,
        out_shape=jax.ShapeDtypeStruct((ids.shape[0],) + blocks.shape[1:], blocks.dtype),
        name="pick_blocks",
    )(ids, blocks)


def fill_kernel(parts_ref, buffer_ref, out_ref, sum_ref, sems):
    sum_ref[...] = jnp.sum(parts_ref[...].astype(f32), axis=0).astype(bf16)
    groups, rows, width = out_ref.shape
    lead = sum_ref.shape[0]
    copies = [
        pltpu.make_async_copy(
            sum_ref, out_ref.at[g, pl.ds(rows - lead, lead), :], sems.at[g]
        )
        for g in range(groups)
    ]
    for copy in copies:
        copy.start()
    for copy in copies:
        copy.wait()


def fill_tail(parts, buffer):
    groups = buffer.shape[0]
    return pl.pallas_call(
        fill_kernel,
        in_specs=[VMEM_SPEC, pl.BlockSpec(memory_space=pl.ANY)],
        out_specs=pl.BlockSpec(memory_space=pl.ANY),
        out_shape=jax.ShapeDtypeStruct(buffer.shape, buffer.dtype),
        scratch_shapes=[
            pltpu.VMEM(parts.shape[1:], bf16),
            pltpu.SemaphoreType.DMA((groups,)),
        ],
        input_output_aliases={1: 0},
        name="fill_tail",
    )(parts, buffer)


def collect_kernel(ids_ref, parts_ref, out_ref, acc_ref):
    shards, rows, width = out_ref.shape
    blocks, blk, _ = acc_ref.shape
    share = blocks * blk // shards
    lead = rows - share
    groups = parts_ref.shape[0]
    acc_ref[...] = jnp.zeros_like(acc_ref)
    total = jnp.zeros((lead, width), f32)
    for g in range(groups):
        acc_ref[ids_ref[g]] += parts_ref[g, 0:blk, :].astype(f32)
        total += parts_ref[g, blk : blk + lead, :].astype(f32)
    total = (total * (1.0 / (groups * shards))).astype(bf16)
    for s in range(shards):
        at = s * share
        out_ref[s, 0:share, :] = acc_ref[at // blk, at % blk : at % blk + share, :].astype(
            bf16
        )
        out_ref[s, share:rows, :] = total


def collect_blocks(ids, parts, blocks, shards):
    groups, rows, width = parts.shape
    share = blocks * BLK // shards
    return pl.pallas_call(
        collect_kernel,
        in_specs=[SMEM_SPEC, VMEM_SPEC],
        out_specs=VMEM_SPEC,
        out_shape=jax.ShapeDtypeStruct((shards, share + rows - BLK, width), bf16),
        scratch_shapes=[pltpu.VMEM((blocks, BLK, width), f32)],
        name="collect_blocks",
    )(ids, parts)


def finish_kernel(parts_ref, machine_ref, *grad_refs):
    shards, rows, width = parts_ref.shape
    share = machine_ref.shape[0]
    lead = rows - share
    total = jnp.zeros((share, width), f32)
    for s in range(shards):
        total += parts_ref[s, 0:share, :].astype(f32)
        at = s * lead
        while at < (s + 1) * lead:
            which, row = at // width, at % width
            size = min((s + 1) * lead - at, width - row)
            start = share + at - s * lead
            grad_refs[which][row : row + size, :] = parts_ref[
                s, start : start + size, :
            ].astype(f32)
            at += size
    machine_ref[...] = total


def finish(parts, share):
    width = parts.shape[2]
    square = jax.ShapeDtypeStruct((width, width), f32)
    return pl.pallas_call(
        finish_kernel,
        in_specs=[VMEM_SPEC],
        out_specs=[VMEM_SPEC] * 4,
        out_shape=[jax.ShapeDtypeStruct((share, width), f32), square, square, square],
        name="finish",
    )(parts)


def swap(x, axis):
    return lax.all_to_all(x, axis, split_axis=0, concat_axis=0, tiled=True)


def per_device(op_embed, machine_embed, cotangent, w_query, w_key, w_value, slot_local, counts):
    groups = lax.axis_size("grp")
    shards = lax.axis_size("ops")
    width = op_embed.shape[1]
    machine_rows = machine_embed.shape[0]
    blocks_here = machine_rows // BLK
    ids = swap(slot_local.reshape(groups, 1), "grp")[:, 0]
    outgoing = pick_blocks(ids, machine_embed.reshape(blocks_here, BLK, width))
    rows = swap(outgoing, "grp")
    lead = 3 * width // shards
    back, op_grad, wgrad = attend(
        rows, counts.T, op_embed, cotangent, w_query, w_key, w_value, extra=lead
    )
    scattered = swap(wgrad.reshape(shards, lead, width), "ops")
    returned = swap(fill_tail(scattered, back), "grp")
    shares = swap(collect_blocks(ids, returned, blocks_here, shards), "ops")
    machine_grad, grad_wq, grad_wk, grad_wv = finish(shares, machine_rows // shards)
    return (op_grad, machine_grad, grad_wq, grad_wk, grad_wv)


def solution(mesh):
    return jax.shard_map(
        per_device,
        mesh=mesh,
        in_specs=(
            P(("grp", "ops"), None),
            P("grp", None),
            P(("grp", "ops"), None),
            P(),
            P(),
            P(),
            P(("grp", "ops"), None),
            P(("grp", "ops"), None),
        ),
        out_specs=(P(("grp", "ops"), None), P(("grp", "ops"), None), P(), P(), P()),
        check_vma=False,
    )
```

```python
import jax
import jax.numpy as jnp
from jax import lax
from jax.experimental import pallas as pl
from jax.experimental.pallas import tpu as pltpu
from jax.sharding import PartitionSpec as P


HEADS = 8
BLK = 128
X_SIZE = 4
Z_SIZE = 8
MEAN_SCALE = 0.08838834764831845

f32 = jnp.float32
bf16 = jnp.bfloat16
VMEM_SPEC = pl.BlockSpec(memory_space=pltpu.VMEM)
SMEM_SPEC = pl.BlockSpec(memory_space=pltpu.SMEM)


def dot(a, b):
    return jnp.dot(a, b, preferred_element_type=f32)


def dot_nt(a, b):
    return lax.dot_general(a, b, (((1,), (1,)), ((), ())), preferred_element_type=f32)


def dot_tt(a, b):
    return lax.dot_general(a, b, (((0,), (1,)), ((), ())), preferred_element_type=f32)


def dot_tn(a, b):
    return lax.dot_general(a, b, (((0,), (0,)), ((), ())), preferred_element_type=f32)


def attend_kernel(
    place_ref,
    rows_ref,
    counts_ref,
    op_ref,
    cot_ref,
    wq_ref,
    wk_ref,
    wv_ref,
    wkt_ref,
    back_ref,
    opg_ref,
    own_ref,
    *rest,
):
    send_refs, (qm_ref, cm_ref, gq_ref, wkv_ref, ct_ref, wgrad_ref) = rest[:-6], rest[-6:]
    slots, blk, width = rows_ref.shape
    ops_count = op_ref.shape[0]
    head_size = width // HEADS
    inv_root = head_size ** (-0.5)
    d_scale = 0.25 * MEAN_SCALE * inv_root
    pair = 8
    machines = pair * blk

    queries = dot(op_ref[...], wq_ref[...]).astype(bf16)
    cot = cot_ref[...]
    ct_ref[...] = cot.T
    lane_head = lax.broadcasted_iota(jnp.int32, (ops_count, width), 1) // head_size
    zero = jnp.zeros((), bf16)
    for h in range(HEADS):
        here = lane_head == h
        qm_ref[pl.ds(h * ops_count, ops_count), :] = jnp.where(here, queries, zero)
        cm_ref[pl.ds(h * ops_count, ops_count), :] = jnp.where(here, cot, zero)
    gq_ref[...] = jnp.zeros_like(gq_ref)
    wkv_ref[...] = jnp.zeros_like(wkv_ref)

    def one_pair(step, carry):
        first = step * pair
        embed = rows_ref[pl.ds(first, pair)].reshape(machines, width)
        keys = dot(embed, wk_ref[...]).astype(bf16)
        values = dot(embed, wv_ref[...]).astype(bf16)
        keys_t = keys.T
        place = lax.broadcasted_iota(jnp.int32, (blk, ops_count), 0)
        eligible = jnp.concatenate(
            [place < counts_ref[first + s] for s in range(pair)], axis=0
        )
        key_grad = jnp.zeros((machines, width), f32)
        value_grad = []
        for h in range(HEADS):
            q_h = qm_ref[pl.ds(h * ops_count, ops_count), :]
            c_h = cm_ref[pl.ds(h * ops_count, ops_count), :]
            scores = dot_nt(keys, q_h)
            value_dot = dot_nt(values, c_h)
            half = jnp.tanh(scores * (0.5 * inv_root))
            gate2 = jnp.where(eligible, 1.0 + half, 0.0).astype(bf16)
            slope = jnp.where(eligible, value_dot * (1.0 - half * half), 0.0).astype(bf16)
            key_grad += dot(slope, q_h)
            value_grad.append(dot_nt(ct_ref[h * head_size : (h + 1) * head_size, :], gate2))
            gq_ref[pl.ds(h * head_size, head_size), :] += dot(
                keys_t[h * head_size : (h + 1) * head_size, :], slope
            )
        key_grad = (key_grad * d_scale).astype(bf16)
        value_grad = (jnp.concatenate(value_grad, axis=0) * (0.5 * MEAN_SCALE)).astype(bf16)
        back = dot_nt(key_grad, wk_ref[...]) + dot_tt(value_grad, wv_ref[...])
        back = back.astype(bf16)
        for s in range(pair):
            back_ref[first + s, 0:blk, :] = back[s * blk : (s + 1) * blk]
        wkv_ref[0:width, :] += dot_tn(embed, key_grad)
        wkv_ref[width : 2 * width, :] += dot(value_grad, embed)
        return carry

    lax.fori_loop(0, slots // pair, one_pair, 0)
    grad_query = (gq_ref[...] * d_scale).T.astype(bf16)
    opg_ref[...] = (cot.astype(f32) + dot_nt(grad_query, wq_ref[...])).astype(bf16)
    wgrad_ref[0:width, :] = dot_tn(op_ref[...], grad_query)
    wgrad_ref[width : 2 * width, :] = wkv_ref[0:width, :]
    wgrad_ref[2 * width : 3 * width, :] = wkv_ref[width : 2 * width, :].T
    part = own_ref.shape[0]
    own_ref[...] = wgrad_ref[pl.ds(pl.multiple_of(place_ref[0] * part, 8), part), :]
    for d, send_ref in enumerate(send_refs):
        other = lax.rem(place_ref[0] + d + 1, len(send_refs) + 1)
        send_ref[...] = wgrad_ref[pl.ds(pl.multiple_of(other * part, 8), part), :].astype(bf16)


def attend(place, rows, counts_t, op_embed, cotangent, w_query, w_key, w_value):
    slots, blk, width = rows.shape
    ops_count = op_embed.shape[0]
    part = 3 * width // X_SIZE
    return pl.pallas_call(
        attend_kernel,
        in_specs=[SMEM_SPEC] + [VMEM_SPEC] * 8,
        out_specs=[VMEM_SPEC] * (2 + X_SIZE),
        out_shape=[
            jax.ShapeDtypeStruct((slots, blk, width), bf16),
            jax.ShapeDtypeStruct((ops_count, width), bf16),
            jax.ShapeDtypeStruct((part, width), f32),
        ]
        + [jax.ShapeDtypeStruct((part, width), bf16)] * (X_SIZE - 1),
        scratch_shapes=[
            pltpu.VMEM((HEADS * ops_count, width), bf16),
            pltpu.VMEM((HEADS * ops_count, width), bf16),
            pltpu.VMEM((width, ops_count), f32),
            pltpu.VMEM((2 * width, width), f32),
            pltpu.VMEM((width, ops_count), bf16),
            pltpu.VMEM((3 * width, width), f32),
        ],
        name="attend",
    )(
        place,
        rows,
        counts_t.reshape(slots, 1, ops_count),
        op_embed,
        cotangent,
        w_query,
        w_key,
        w_value,
        w_key.T,
    )


def fold_kernel(place_ref, own_ref, *refs):
    got, own_out, sends, total_ref = (
        refs[: X_SIZE - 1],
        refs[X_SIZE - 1],
        refs[X_SIZE:-1],
        refs[-1],
    )
    total = own_ref[...]
    for ref in got:
        total += ref[...].astype(f32)
    total_ref[...] = total
    part = own_out.shape[0]
    own_out[...] = total_ref[pl.ds(pl.multiple_of(place_ref[1] * part, 8), part), :]
    for d, send_ref in enumerate(sends):
        other = lax.rem(place_ref[1] + d + 1, Z_SIZE)
        send_ref[...] = total_ref[pl.ds(pl.multiple_of(other * part, 8), part), :]


def fold(place, own, got):
    rows, width = own.shape
    piece = jax.ShapeDtypeStruct((rows // Z_SIZE, width), f32)
    return pl.pallas_call(
        fold_kernel,
        in_specs=[SMEM_SPEC] + [VMEM_SPEC] * X_SIZE,
        out_specs=[VMEM_SPEC] * Z_SIZE,
        out_shape=[piece] * Z_SIZE,
        scratch_shapes=[pltpu.VMEM(own.shape, f32)],
        name="fold",
    )(place, own, *got)


def spread_kernel(*refs):
    out_ref = refs[-1]
    total = refs[0][...]
    for ref in refs[1:-1]:
        total += ref[...]
    total = total.astype(bf16)
    for g in range(out_ref.shape[0]):
        out_ref[g] = total


def spread(pieces, groups):
    return pl.pallas_call(
        spread_kernel,
        in_specs=[VMEM_SPEC] * len(pieces),
        out_specs=VMEM_SPEC,
        out_shape=jax.ShapeDtypeStruct((groups,) + pieces[0].shape, bf16),
        name="spread",
    )(*pieces)


def pick_kernel(ids_ref, blocks_ref, out_ref):
    for g in range(out_ref.shape[0]):
        out_ref[g] = blocks_ref[ids_ref[g]]


def pick_blocks(ids, blocks):
    return pl.pallas_call(
        pick_kernel,
        in_specs=[SMEM_SPEC, VMEM_SPEC],
        out_specs=VMEM_SPEC,
        out_shape=jax.ShapeDtypeStruct((ids.shape[0],) + blocks.shape[1:], blocks.dtype),
        name="pick_blocks",
    )(ids, blocks)


def collect_kernel(ids_ref, parts_ref, lead_ref, out_ref, acc_ref):
    shards, rows, width = out_ref.shape
    blocks, blk, _ = acc_ref.shape
    share = blocks * blk // shards
    lead = rows - share
    groups = parts_ref.shape[0]
    acc_ref[...] = jnp.zeros_like(acc_ref)
    total = jnp.zeros((lead, width), f32)
    for g in range(groups):
        acc_ref[ids_ref[g]] += parts_ref[g].astype(f32)
        total += lead_ref[g].astype(f32)
    total = (total * (1.0 / (groups * shards))).astype(bf16)
    for s in range(shards):
        at = s * share
        out_ref[s, 0:share, :] = acc_ref[at // blk, at % blk : at % blk + share, :].astype(
            bf16
        )
        out_ref[s, share:rows, :] = total


def collect_blocks(ids, parts, leads, blocks, shards):
    width = parts.shape[2]
    rows = blocks * BLK // shards + leads.shape[1]
    return pl.pallas_call(
        collect_kernel,
        in_specs=[SMEM_SPEC, VMEM_SPEC, VMEM_SPEC],
        out_specs=VMEM_SPEC,
        out_shape=jax.ShapeDtypeStruct((shards, rows, width), bf16),
        scratch_shapes=[pltpu.VMEM((blocks, BLK, width), f32)],
        name="collect_blocks",
    )(ids, parts, leads)


def finish_kernel(parts_ref, machine_ref, *grad_refs):
    shards, rows, width = parts_ref.shape
    share = machine_ref.shape[0]
    lead = rows - share
    total = jnp.zeros((share, width), f32)
    for s in range(shards):
        total += parts_ref[s, 0:share, :].astype(f32)
        at = s * lead
        while at < (s + 1) * lead:
            which, row = at // width, at % width
            size = min((s + 1) * lead - at, width - row)
            start = share + at - s * lead
            grad_refs[which][row : row + size, :] = parts_ref[
                s, start : start + size, :
            ].astype(f32)
            at += size
    machine_ref[...] = total


def finish(parts, share):
    width = parts.shape[2]
    square = jax.ShapeDtypeStruct((width, width), f32)
    return pl.pallas_call(
        finish_kernel,
        in_specs=[VMEM_SPEC],
        out_specs=[VMEM_SPEC] * 4,
        out_shape=[jax.ShapeDtypeStruct((share, width), f32), square, square, square],
        name="finish",
    )(parts)


def swap(x, axis):
    return lax.all_to_all(x, axis, split_axis=0, concat_axis=0, tiled=True)


def shift_x(x, d):
    pairs = [
        (i * Z_SIZE + k, (i + d) % X_SIZE * Z_SIZE + k)
        for i in range(X_SIZE)
        for k in range(Z_SIZE)
    ]
    return lax.ppermute(x, "ops", pairs)


def shift_z(x, d):
    pairs = [
        (i * Z_SIZE + k, i * Z_SIZE + (k + d) % Z_SIZE)
        for i in range(X_SIZE)
        for k in range(Z_SIZE)
    ]
    return lax.ppermute(x, "ops", pairs)


def per_device(op_embed, machine_embed, cotangent, w_query, w_key, w_value, slot_local, counts):
    groups = lax.axis_size("grp")
    shards = lax.axis_size("ops")
    width = op_embed.shape[1]
    machine_rows = machine_embed.shape[0]
    blocks_here = machine_rows // BLK
    ids = swap(slot_local.reshape(groups, 1), "grp")[:, 0]
    outgoing = pick_blocks(ids, machine_embed.reshape(blocks_here, BLK, width))
    rows = swap(outgoing, "grp")
    spot = lax.axis_index("ops")
    place = jnp.stack([spot // Z_SIZE, spot % Z_SIZE]).astype(jnp.int32)
    back, op_grad, own, *sends = attend(
        place, rows, counts.T, op_embed, cotangent, w_query, w_key, w_value
    )
    returned = swap(back, "grp")
    got = [shift_x(send, d + 1) for d, send in enumerate(sends)]
    own, *sends = fold(place, own, got)
    got = [shift_z(send, d + 1) for d, send in enumerate(sends)]
    leads = spread([own] + got, groups)
    leads = swap(leads, "grp")
    shares = swap(collect_blocks(ids, returned, leads, blocks_here, shards), "ops")
    machine_grad, grad_wq, grad_wk, grad_wv = finish(shares, machine_rows // shards)
    return (op_grad, machine_grad, grad_wq, grad_wk, grad_wv)


def solution(mesh):
    return jax.shard_map(
        per_device,
        mesh=mesh,
        in_specs=(
            P(("grp", "ops"), None),
            P("grp", None),
            P(("grp", "ops"), None),
            P(),
            P(),
            P(),
            P(("grp", "ops"), None),
            P(("grp", "ops"), None),
        ),
        out_specs=(P(("grp", "ops"), None), P(("grp", "ops"), None), P(), P(), P()),
        check_vma=False,
    )
```

```python
import functools

import jax
import jax.numpy as jnp
from jax import lax
from jax.experimental import pallas as pl
from jax.experimental.pallas import tpu as pltpu
from jax.sharding import PartitionSpec as P

HEADS = 8
BLK = 128
SMALL = 8 << 20
MEAN_SCALE = 0.08838834764831845

f32 = jnp.float32
bf16 = jnp.bfloat16
VMEM_SPEC = pl.BlockSpec(memory_space=pltpu.VMEM)
SMEM_SPEC = pl.BlockSpec(memory_space=pltpu.SMEM)
ANY_SPEC = pl.BlockSpec(memory_space=pl.ANY)


def dot(a, b):
    return jnp.dot(a, b, preferred_element_type=f32)


def dot_nt(a, b):
    return lax.dot_general(a, b, (((1,), (1,)), ((), ())), preferred_element_type=f32)


def dot_tt(a, b):
    return lax.dot_general(a, b, (((0,), (1,)), ((), ())), preferred_element_type=f32)


def dot_tn(a, b):
    return lax.dot_general(a, b, (((0,), (0,)), ((), ())), preferred_element_type=f32)


def attend_kernel(
    rows_ref,
    counts_ref,
    op_ref,
    cot_ref,
    wq_ref,
    wk_ref,
    wv_ref,
    back_ref,
    opg_ref,
    wgrad_ref,
    qm_ref,
    cm_ref,
    gq_ref,
    wkv_ref,
    ct_ref,
):
    slots, blk, width = rows_ref.shape
    ops_count = op_ref.shape[0]
    head_size = width // HEADS
    inv_root = head_size ** (-0.5)
    d_scale = 0.25 * MEAN_SCALE * inv_root
    pair = 8
    machines = pair * blk
    steps = slots // pair

    queries = dot(op_ref[...], wq_ref[...]).astype(bf16)
    cot = cot_ref[...]
    ct_ref[...] = cot.T
    lane_head = lax.broadcasted_iota(jnp.int32, (ops_count, width), 1) // head_size
    zero = jnp.zeros((), bf16)
    for h in range(HEADS):
        here = lane_head == h
        qm_ref[pl.ds(h * ops_count, ops_count), :] = jnp.where(here, queries, zero)
        cm_ref[pl.ds(h * ops_count, ops_count), :] = jnp.where(here, cot, zero)
    gq_ref[...] = jnp.zeros_like(gq_ref)
    wkv_ref[...] = jnp.zeros_like(wkv_ref)

    def one_pair(step, carry):
        first = step * pair
        embed = rows_ref[pl.ds(first, pair)].reshape(machines, width)
        keys = dot(embed, wk_ref[...]).astype(bf16)
        values = dot(embed, wv_ref[...]).astype(bf16)
        keys_t = keys.T
        place = lax.broadcasted_iota(jnp.int32, (blk, ops_count), 0)
        eligible = jnp.concatenate(
            [place < counts_ref[first + s] for s in range(pair)], axis=0
        )
        key_grad = jnp.zeros((machines, width), f32)
        value_grad = []
        for h in range(HEADS):
            q_h = qm_ref[pl.ds(h * ops_count, ops_count), :]
            c_h = cm_ref[pl.ds(h * ops_count, ops_count), :]
            scores = dot_nt(keys, q_h)
            value_dot = dot_nt(values, c_h)
            half = jnp.tanh(scores * (0.5 * inv_root))
            gate2 = jnp.where(eligible, 1.0 + half, 0.0).astype(bf16)
            slope = jnp.where(eligible, value_dot * (1.0 - half * half), 0.0).astype(bf16)
            key_grad += dot(slope, q_h)
            value_grad.append(dot_nt(ct_ref[h * head_size : (h + 1) * head_size, :], gate2))
            gq_ref[pl.ds(h * head_size, head_size), :] += dot(
                keys_t[h * head_size : (h + 1) * head_size, :], slope
            )
        key_grad = (key_grad * d_scale).astype(bf16)
        value_grad = (jnp.concatenate(value_grad, axis=0) * (0.5 * MEAN_SCALE)).astype(bf16)
        back = dot_nt(key_grad, wk_ref[...]) + dot_tt(value_grad, wv_ref[...])
        back = back.astype(bf16)
        for s in range(pair):
            back_ref[first + s, 0:blk, :] = back[s * blk : (s + 1) * blk]
        wkv_ref[0:width, :] += dot_tn(embed, key_grad)
        wkv_ref[width : 2 * width, :] += dot(value_grad, embed)
        return carry

    lax.fori_loop(0, steps, one_pair, 0)
    grad_query = (gq_ref[...] * d_scale).T.astype(bf16)
    opg_ref[...] = (cot.astype(f32) + dot_nt(grad_query, wq_ref[...])).astype(bf16)
    wgrad_ref[0:width, :] = dot_tn(op_ref[...], grad_query).astype(bf16)
    wgrad_ref[width : 2 * width, :] = wkv_ref[0:width, :].astype(bf16)
    wgrad_ref[2 * width : 3 * width, :] = wkv_ref[width : 2 * width, :].T.astype(bf16)


def attend(rows, counts_t, op_embed, cotangent, w_query, w_key, w_value, extra=0):
    slots, blk, width = rows.shape
    ops_count = op_embed.shape[0]
    return pl.pallas_call(
        attend_kernel,
        in_specs=[VMEM_SPEC] * 7,
        out_specs=[VMEM_SPEC] * 3,
        out_shape=[
            jax.ShapeDtypeStruct((slots, blk + extra, width), bf16),
            jax.ShapeDtypeStruct((ops_count, width), bf16),
            jax.ShapeDtypeStruct((3 * width, width), bf16),
        ],
        scratch_shapes=[
            pltpu.VMEM((HEADS * ops_count, width), bf16),
            pltpu.VMEM((HEADS * ops_count, width), bf16),
            pltpu.VMEM((width, ops_count), f32),
            pltpu.VMEM((2 * width, width), f32),
            pltpu.VMEM((width, ops_count), bf16),
        ],
        compiler_params=pltpu.CompilerParams(vmem_limit_bytes=48 << 20),
        name="attend",
    )(
        rows,
        counts_t.reshape(slots, 1, ops_count),
        op_embed,
        cotangent,
        w_query,
        w_key,
        w_value,
    )


def pick_kernel(ids_ref, blocks_ref, out_ref, held, in_sem, out_sems):
    load = pltpu.make_async_copy(blocks_ref, held, in_sem)
    load.start()
    load.wait()
    copies = [
        pltpu.make_async_copy(held.at[ids_ref[g, 0, 0]], out_ref.at[g], out_sems.at[g])
        for g in range(out_ref.shape[0])
    ]
    for copy in copies:
        copy.start()
    for copy in copies:
        copy.wait()


def pick_blocks(ids, blocks):
    groups = ids.shape[0]
    return pl.pallas_call(
        pick_kernel,
        in_specs=[SMEM_SPEC, ANY_SPEC],
        out_specs=ANY_SPEC,
        out_shape=jax.ShapeDtypeStruct((groups,) + blocks.shape[1:], blocks.dtype),
        scratch_shapes=[
            pltpu.VMEM(blocks.shape, blocks.dtype),
            pltpu.SemaphoreType.DMA,
            pltpu.SemaphoreType.DMA((groups,)),
        ],
        compiler_params=pltpu.CompilerParams(vmem_limit_bytes=SMALL),
        name="pick_blocks",
    )(ids, blocks)


def fill_kernel(parts_ref, buffer_ref, out_ref, sum_ref, sems):
    sum_ref[...] = jnp.sum(parts_ref[...].astype(f32), axis=0).astype(bf16)
    groups, rows, width = out_ref.shape
    lead = sum_ref.shape[0]
    copies = [
        pltpu.make_async_copy(
            sum_ref, out_ref.at[g, pl.ds(rows - lead, lead), :], sems.at[g]
        )
        for g in range(groups)
    ]
    for copy in copies:
        copy.start()
    for copy in copies:
        copy.wait()


def fill_tail(parts, buffer):
    groups = buffer.shape[0]
    return pl.pallas_call(
        fill_kernel,
        in_specs=[VMEM_SPEC, pl.BlockSpec(memory_space=pl.ANY)],
        out_specs=pl.BlockSpec(memory_space=pl.ANY),
        out_shape=jax.ShapeDtypeStruct(buffer.shape, buffer.dtype),
        scratch_shapes=[
            pltpu.VMEM(parts.shape[1:], bf16),
            pltpu.SemaphoreType.DMA((groups,)),
        ],
        input_output_aliases={1: 0},
        compiler_params=pltpu.CompilerParams(vmem_limit_bytes=SMALL),
        name="fill_tail",
    )(parts, buffer)


def collect_kernel(ids_ref, parts_ref, out_ref, acc_ref):
    shards, rows, width = out_ref.shape
    blocks, blk, _ = acc_ref.shape
    share = blocks * blk // shards
    lead = rows - share
    groups = parts_ref.shape[0]
    acc_ref[...] = jnp.zeros_like(acc_ref)
    total = jnp.zeros((lead, width), f32)
    for g in range(groups):
        acc_ref[ids_ref[g, 0, 0]] += parts_ref[g, 0:blk, :].astype(f32)
        total += parts_ref[g, blk : blk + lead, :].astype(f32)
    total = (total * (1.0 / (groups * shards))).astype(bf16)
    for s in range(shards):
        at = s * share
        out_ref[s, 0:share, :] = acc_ref[at // blk, at % blk : at % blk + share, :].astype(
            bf16
        )
        out_ref[s, share:rows, :] = total


def collect_blocks(ids, parts, blocks, shards):
    groups, rows, width = parts.shape
    share = blocks * BLK // shards
    return pl.pallas_call(
        collect_kernel,
        in_specs=[SMEM_SPEC, VMEM_SPEC],
        out_specs=VMEM_SPEC,
        out_shape=jax.ShapeDtypeStruct((shards, share + rows - BLK, width), bf16),
        scratch_shapes=[pltpu.VMEM((blocks, BLK, width), f32)],
        compiler_params=pltpu.CompilerParams(vmem_limit_bytes=SMALL),
        name="collect_blocks",
    )(ids, parts)


def finish_kernel(parts_ref, machine_ref, *grad_refs):
    shards, rows, width = parts_ref.shape
    share = machine_ref.shape[0]
    lead = rows - share
    total = jnp.zeros((share, width), f32)
    for s in range(shards):
        total += parts_ref[s, 0:share, :].astype(f32)
        at = s * lead
        while at < (s + 1) * lead:
            which, row = at // width, at % width
            size = min((s + 1) * lead - at, width - row)
            start = share + at - s * lead
            grad_refs[which][row : row + size, :] = parts_ref[
                s, start : start + size, :
            ].astype(f32)
            at += size
    machine_ref[...] = total


def finish(parts, share):
    width = parts.shape[2]
    square = jax.ShapeDtypeStruct((width, width), f32)
    return pl.pallas_call(
        finish_kernel,
        in_specs=[VMEM_SPEC],
        out_specs=[VMEM_SPEC] * 4,
        out_shape=[jax.ShapeDtypeStruct((share, width), f32), square, square, square],
        compiler_params=pltpu.CompilerParams(vmem_limit_bytes=SMALL),
        name="finish",
    )(parts)


def swap(x, axis):
    return lax.all_to_all(x, axis, split_axis=0, concat_axis=0, tiled=True)


def per_device(op_embed, machine_embed, cotangent, w_query, w_key, w_value, slot_local, counts):
    groups = lax.axis_size("grp")
    shards = lax.axis_size("ops")
    width = op_embed.shape[1]
    machine_rows = machine_embed.shape[0]
    blocks_here = machine_rows // BLK
    ids = swap(jnp.broadcast_to(slot_local.reshape(groups, 1, 1), (groups, 1, 128)), "grp")
    outgoing = pick_blocks(ids, machine_embed.reshape(blocks_here, BLK, width))
    rows = swap(outgoing, "grp")
    lead = 3 * width // shards
    back, op_grad, wgrad = attend(
        rows, counts.T, op_embed, cotangent, w_query, w_key, w_value, extra=lead
    )
    scattered = swap(wgrad.reshape(shards, lead, width), "ops")
    returned = swap(fill_tail(scattered, back), "grp")
    shares = swap(collect_blocks(ids, returned, blocks_here, shards), "ops")
    machine_grad, grad_wq, grad_wk, grad_wv = finish(shares, machine_rows // shards)
    return (op_grad, machine_grad, grad_wq, grad_wk, grad_wv)


def solution(mesh):
    return jax.shard_map(
        per_device,
        mesh=mesh,
        in_specs=(
            P(("grp", "ops"), None),
            P("grp", None),
            P(("grp", "ops"), None),
            P(),
            P(),
            P(),
            P(("grp", "ops"), None),
            P(("grp", "ops"), None),
        ),
        out_specs=(P(("grp", "ops"), None), P(("grp", "ops"), None), P(), P(), P()),
        check_vma=False,
    )
```

```python
import functools

import jax
import jax.numpy as jnp
from jax import lax
from jax.experimental import pallas as pl
from jax.experimental.pallas import tpu as pltpu
from jax.sharding import PartitionSpec as P

HEADS = 8
BLK = 128
SMALL = 8 << 20
MEAN_SCALE = 0.08838834764831845

f32 = jnp.float32
bf16 = jnp.bfloat16
VMEM_SPEC = pl.BlockSpec(memory_space=pltpu.VMEM)
SMEM_SPEC = pl.BlockSpec(memory_space=pltpu.SMEM)
ANY_SPEC = pl.BlockSpec(memory_space=pl.ANY)


def dot(a, b):
    return jnp.dot(a, b, preferred_element_type=f32)


def dot_nt(a, b):
    return lax.dot_general(a, b, (((1,), (1,)), ((), ())), preferred_element_type=f32)


def dot_tt(a, b):
    return lax.dot_general(a, b, (((0,), (1,)), ((), ())), preferred_element_type=f32)


def dot_tn(a, b):
    return lax.dot_general(a, b, (((0,), (0,)), ((), ())), preferred_element_type=f32)


def attend_kernel(
    rows_ref,
    counts_ref,
    op_ref,
    cot_ref,
    wq_ref,
    wk_ref,
    wv_ref,
    back_ref,
    opg_ref,
    wgrad_ref,
    qm_ref,
    cm_ref,
    gq_ref,
    wkv_ref,
    ct_ref,
):
    slots, blk, width = rows_ref.shape
    ops_count = op_ref.shape[0]
    head_size = width // HEADS
    inv_root = head_size ** (-0.5)
    d_scale = 0.25 * MEAN_SCALE * inv_root
    pair = 16
    machines = pair * blk
    steps = slots // pair

    queries = dot(op_ref[...], wq_ref[...]).astype(bf16)
    cot = cot_ref[...]
    ct_ref[...] = cot.T
    lane_head = lax.broadcasted_iota(jnp.int32, (ops_count, width), 1) // head_size
    zero = jnp.zeros((), bf16)
    for h in range(HEADS):
        here = lane_head == h
        qm_ref[pl.ds(h * ops_count, ops_count), :] = jnp.where(here, queries, zero)
        cm_ref[pl.ds(h * ops_count, ops_count), :] = jnp.where(here, cot, zero)
    gq_ref[...] = jnp.zeros_like(gq_ref)
    wkv_ref[...] = jnp.zeros_like(wkv_ref)

    def one_pair(step, carry):
        first = step * pair
        embed = rows_ref[pl.ds(first, pair)].reshape(machines, width)
        keys = dot(embed, wk_ref[...]).astype(bf16)
        values = dot(embed, wv_ref[...]).astype(bf16)
        keys_t = keys.T
        place = lax.broadcasted_iota(jnp.int32, (blk, ops_count), 0)
        eligible = jnp.concatenate(
            [place < counts_ref[first + s] for s in range(pair)], axis=0
        )
        key_grad = jnp.zeros((machines, width), f32)
        value_grad = []
        for h in range(HEADS):
            q_h = qm_ref[pl.ds(h * ops_count, ops_count), :]
            c_h = cm_ref[pl.ds(h * ops_count, ops_count), :]
            scores = dot_nt(keys, q_h)
            value_dot = dot_nt(values, c_h)
            half = jnp.tanh(scores * (0.5 * inv_root))
            gate2 = jnp.where(eligible, 1.0 + half, 0.0).astype(bf16)
            slope = jnp.where(eligible, value_dot * (1.0 - half * half), 0.0).astype(bf16)
            key_grad += dot(slope, q_h)
            value_grad.append(dot_nt(ct_ref[h * head_size : (h + 1) * head_size, :], gate2))
            gq_ref[pl.ds(h * head_size, head_size), :] += dot(
                keys_t[h * head_size : (h + 1) * head_size, :], slope
            )
        key_grad = (key_grad * d_scale).astype(bf16)
        value_grad = (jnp.concatenate(value_grad, axis=0) * (0.5 * MEAN_SCALE)).astype(bf16)
        back = dot_nt(key_grad, wk_ref[...]) + dot_tt(value_grad, wv_ref[...])
        back = back.astype(bf16)
        for s in range(pair):
            back_ref[first + s, 0:blk, :] = back[s * blk : (s + 1) * blk]
        wkv_ref[0:width, :] += dot_tn(embed, key_grad)
        wkv_ref[width : 2 * width, :] += dot(value_grad, embed)
        return carry

    lax.fori_loop(0, steps, one_pair, 0)
    grad_query = (gq_ref[...] * d_scale).T.astype(bf16)
    opg_ref[...] = (cot.astype(f32) + dot_nt(grad_query, wq_ref[...])).astype(bf16)
    wgrad_ref[0:width, :] = dot_tn(op_ref[...], grad_query).astype(bf16)
    wgrad_ref[width : 2 * width, :] = wkv_ref[0:width, :].astype(bf16)
    wgrad_ref[2 * width : 3 * width, :] = wkv_ref[width : 2 * width, :].T.astype(bf16)


def attend(rows, counts_t, op_embed, cotangent, w_query, w_key, w_value, extra=0):
    slots, blk, width = rows.shape
    ops_count = op_embed.shape[0]
    return pl.pallas_call(
        attend_kernel,
        in_specs=[VMEM_SPEC] * 7,
        out_specs=[VMEM_SPEC] * 3,
        out_shape=[
            jax.ShapeDtypeStruct((slots, blk + extra, width), bf16),
            jax.ShapeDtypeStruct((ops_count, width), bf16),
            jax.ShapeDtypeStruct((3 * width, width), bf16),
        ],
        scratch_shapes=[
            pltpu.VMEM((HEADS * ops_count, width), bf16),
            pltpu.VMEM((HEADS * ops_count, width), bf16),
            pltpu.VMEM((width, ops_count), f32),
            pltpu.VMEM((2 * width, width), f32),
            pltpu.VMEM((width, ops_count), bf16),
        ],
        compiler_params=pltpu.CompilerParams(vmem_limit_bytes=48 << 20),
        name="attend",
    )(
        rows,
        counts_t.reshape(slots, 1, ops_count),
        op_embed,
        cotangent,
        w_query,
        w_key,
        w_value,
    )


def pick_kernel(ids_ref, blocks_ref, out_ref, held, in_sem, out_sems):
    load = pltpu.make_async_copy(blocks_ref, held, in_sem)
    load.start()
    load.wait()
    copies = [
        pltpu.make_async_copy(held.at[ids_ref[g, 0, 0]], out_ref.at[g], out_sems.at[g])
        for g in range(out_ref.shape[0])
    ]
    for copy in copies:
        copy.start()
    for copy in copies:
        copy.wait()


def pick_blocks(ids, blocks):
    groups = ids.shape[0]
    return pl.pallas_call(
        pick_kernel,
        in_specs=[SMEM_SPEC, ANY_SPEC],
        out_specs=ANY_SPEC,
        out_shape=jax.ShapeDtypeStruct((groups,) + blocks.shape[1:], blocks.dtype),
        scratch_shapes=[
            pltpu.VMEM(blocks.shape, blocks.dtype),
            pltpu.SemaphoreType.DMA,
            pltpu.SemaphoreType.DMA((groups,)),
        ],
        compiler_params=pltpu.CompilerParams(vmem_limit_bytes=60 << 20),
        name="pick_blocks",
    )(ids, blocks)


def fill_kernel(parts_ref, buffer_ref, out_ref, sum_ref, sems):
    sum_ref[...] = jnp.sum(parts_ref[...].astype(f32), axis=0).astype(bf16)
    groups, rows, width = out_ref.shape
    lead = sum_ref.shape[0]
    copies = [
        pltpu.make_async_copy(
            sum_ref, out_ref.at[g, pl.ds(rows - lead, lead), :], sems.at[g]
        )
        for g in range(groups)
    ]
    for copy in copies:
        copy.start()
    for copy in copies:
        copy.wait()


def fill_tail(parts, buffer):
    groups = buffer.shape[0]
    return pl.pallas_call(
        fill_kernel,
        in_specs=[VMEM_SPEC, pl.BlockSpec(memory_space=pl.ANY)],
        out_specs=pl.BlockSpec(memory_space=pl.ANY),
        out_shape=jax.ShapeDtypeStruct(buffer.shape, buffer.dtype),
        scratch_shapes=[
            pltpu.VMEM(parts.shape[1:], bf16),
            pltpu.SemaphoreType.DMA((groups,)),
        ],
        input_output_aliases={1: 0},
        compiler_params=pltpu.CompilerParams(vmem_limit_bytes=SMALL),
        name="fill_tail",
    )(parts, buffer)


def collect_kernel(ids_ref, parts_ref, out_ref, acc_ref):
    shards, rows, width = out_ref.shape
    blocks, blk, _ = acc_ref.shape
    share = blocks * blk // shards
    lead = rows - share
    groups = parts_ref.shape[0]
    acc_ref[...] = jnp.zeros_like(acc_ref)
    total = jnp.zeros((lead, width), f32)
    for g in range(groups):
        acc_ref[ids_ref[g, 0, 0]] += parts_ref[g, 0:blk, :].astype(f32)
        total += parts_ref[g, blk : blk + lead, :].astype(f32)
    total = (total * (1.0 / (groups * shards))).astype(bf16)
    for s in range(shards):
        at = s * share
        out_ref[s, 0:share, :] = acc_ref[at // blk, at % blk : at % blk + share, :].astype(
            bf16
        )
        out_ref[s, share:rows, :] = total


def collect_blocks(ids, parts, blocks, shards):
    groups, rows, width = parts.shape
    share = blocks * BLK // shards
    return pl.pallas_call(
        collect_kernel,
        in_specs=[SMEM_SPEC, VMEM_SPEC],
        out_specs=VMEM_SPEC,
        out_shape=jax.ShapeDtypeStruct((shards, share + rows - BLK, width), bf16),
        scratch_shapes=[pltpu.VMEM((blocks, BLK, width), f32)],
        compiler_params=pltpu.CompilerParams(vmem_limit_bytes=SMALL),
        name="collect_blocks",
    )(ids, parts)


def finish_kernel(parts_ref, machine_ref, *grad_refs):
    shards, rows, width = parts_ref.shape
    share = machine_ref.shape[0]
    lead = rows - share
    total = jnp.zeros((share, width), f32)
    for s in range(shards):
        total += parts_ref[s, 0:share, :].astype(f32)
        at = s * lead
        while at < (s + 1) * lead:
            which, row = at // width, at % width
            size = min((s + 1) * lead - at, width - row)
            start = share + at - s * lead
            grad_refs[which][row : row + size, :] = parts_ref[
                s, start : start + size, :
            ].astype(f32)
            at += size
    machine_ref[...] = total


def finish(parts, share):
    width = parts.shape[2]
    square = jax.ShapeDtypeStruct((width, width), f32)
    return pl.pallas_call(
        finish_kernel,
        in_specs=[VMEM_SPEC],
        out_specs=[VMEM_SPEC] * 4,
        out_shape=[jax.ShapeDtypeStruct((share, width), f32), square, square, square],
        compiler_params=pltpu.CompilerParams(vmem_limit_bytes=SMALL),
        name="finish",
    )(parts)


def swap(x, axis):
    return lax.all_to_all(x, axis, split_axis=0, concat_axis=0, tiled=True)


def per_device(op_embed, machine_embed, cotangent, w_query, w_key, w_value, slot_local, counts):
    groups = lax.axis_size("grp")
    shards = lax.axis_size("ops")
    width = op_embed.shape[1]
    machine_rows = machine_embed.shape[0]
    blocks_here = machine_rows // BLK
    ids = swap(jnp.broadcast_to(slot_local.reshape(groups, 1, 1), (groups, 1, 128)), "grp")
    outgoing = pick_blocks(ids, machine_embed.reshape(blocks_here, BLK, width))
    rows = swap(outgoing, "grp")
    lead = 3 * width // shards
    back, op_grad, wgrad = attend(
        rows, counts.T, op_embed, cotangent, w_query, w_key, w_value, extra=lead
    )
    scattered = swap(wgrad.reshape(shards, lead, width), "ops")
    returned = swap(fill_tail(scattered, back), "grp")
    shares = swap(collect_blocks(ids, returned, blocks_here, shards), "ops")
    machine_grad, grad_wq, grad_wk, grad_wv = finish(shares, machine_rows // shards)
    return (op_grad, machine_grad, grad_wq, grad_wk, grad_wv)


def solution(mesh):
    return jax.shard_map(
        per_device,
        mesh=mesh,
        in_specs=(
            P(("grp", "ops"), None),
            P("grp", None),
            P(("grp", "ops"), None),
            P(),
            P(),
            P(),
            P(("grp", "ops"), None),
            P(("grp", "ops"), None),
        ),
        out_specs=(P(("grp", "ops"), None), P(("grp", "ops"), None), P(), P(), P()),
        check_vma=False,
    )
```

```python
import functools

import jax
import jax.numpy as jnp
from jax import lax
from jax.experimental import pallas as pl
from jax.experimental.pallas import tpu as pltpu
from jax.sharding import PartitionSpec as P

HEADS = 8
BLK = 128
SMALL = 8 << 20
MEAN_SCALE = 0.08838834764831845

f32 = jnp.float32
bf16 = jnp.bfloat16
VMEM_SPEC = pl.BlockSpec(memory_space=pltpu.VMEM)
SMEM_SPEC = pl.BlockSpec(memory_space=pltpu.SMEM)
ANY_SPEC = pl.BlockSpec(memory_space=pl.ANY)


def dot(a, b):
    return jnp.dot(a, b, preferred_element_type=f32)


def dot_nt(a, b):
    return lax.dot_general(a, b, (((1,), (1,)), ((), ())), preferred_element_type=f32)


def dot_tt(a, b):
    return lax.dot_general(a, b, (((0,), (1,)), ((), ())), preferred_element_type=f32)


def dot_tn(a, b):
    return lax.dot_general(a, b, (((0,), (0,)), ((), ())), preferred_element_type=f32)


def attend_kernel(
    rows_ref,
    counts_ref,
    op_ref,
    cot_ref,
    wq_ref,
    wk_ref,
    wv_ref,
    back_ref,
    opg_ref,
    wgrad_ref,
    qm_ref,
    cm_ref,
    gq_ref,
    wkv_ref,
    ct_ref,
):
    slots, blk, width = rows_ref.shape
    ops_count = op_ref.shape[0]
    head_size = width // HEADS
    inv_root = head_size ** (-0.5)
    d_scale = 0.25 * MEAN_SCALE * inv_root
    pair = 16
    machines = pair * blk
    steps = slots // pair

    queries = dot(op_ref[...], wq_ref[...]).astype(bf16)
    cot = cot_ref[...]
    ct_ref[...] = cot.T
    lane_head = lax.broadcasted_iota(jnp.int32, (ops_count, width), 1) // head_size
    zero = jnp.zeros((), bf16)
    for h in range(HEADS):
        here = lane_head == h
        qm_ref[pl.ds(h * ops_count, ops_count), :] = jnp.where(here, queries, zero)
        cm_ref[pl.ds(h * ops_count, ops_count), :] = jnp.where(here, cot, zero)
    gq_ref[...] = jnp.zeros_like(gq_ref)
    wkv_ref[...] = jnp.zeros_like(wkv_ref)

    def one_pair(step, carry):
        first = step * pair
        embed = rows_ref[pl.ds(first, pair)].reshape(machines, width)
        keys = dot(embed, wk_ref[...]).astype(bf16)
        values = dot(embed, wv_ref[...]).astype(bf16)
        keys_t = keys.T
        place = lax.broadcasted_iota(jnp.int32, (blk, ops_count), 0)
        eligible = jnp.concatenate(
            [place < counts_ref[first + s : first + s + 1, :] for s in range(pair)], axis=0
        )
        key_grad = jnp.zeros((machines, width), f32)
        value_grad = []
        for h in range(HEADS):
            q_h = qm_ref[pl.ds(h * ops_count, ops_count), :]
            c_h = cm_ref[pl.ds(h * ops_count, ops_count), :]
            scores = dot_nt(keys, q_h)
            value_dot = dot_nt(values, c_h)
            half = jnp.tanh(scores * (0.5 * inv_root))
            gate2 = jnp.where(eligible, 1.0 + half, 0.0).astype(bf16)
            slope = jnp.where(eligible, value_dot * (1.0 - half * half), 0.0).astype(bf16)
            key_grad += dot(slope, q_h)
            value_grad.append(dot_nt(ct_ref[h * head_size : (h + 1) * head_size, :], gate2))
            gq_ref[pl.ds(h * head_size, head_size), :] += dot(
                keys_t[h * head_size : (h + 1) * head_size, :], slope
            )
        key_grad = (key_grad * d_scale).astype(bf16)
        value_grad = (jnp.concatenate(value_grad, axis=0) * (0.5 * MEAN_SCALE)).astype(bf16)
        back = dot_nt(key_grad, wk_ref[...]) + dot_tt(value_grad, wv_ref[...])
        back = back.astype(bf16)
        for s in range(pair):
            back_ref[first + s, 0:blk, :] = back[s * blk : (s + 1) * blk]
        wkv_ref[0:width, :] += dot_tn(embed, key_grad)
        wkv_ref[width : 2 * width, :] += dot(value_grad, embed)
        return carry

    for step in range(steps):
        one_pair(step, 0)
    grad_query = (gq_ref[...] * d_scale).T.astype(bf16)
    opg_ref[...] = (cot.astype(f32) + dot_nt(grad_query, wq_ref[...])).astype(bf16)
    wgrad_ref[0:width, :] = dot_tn(op_ref[...], grad_query).astype(bf16)
    wgrad_ref[width : 2 * width, :] = wkv_ref[0:width, :].astype(bf16)
    wgrad_ref[2 * width : 3 * width, :] = wkv_ref[width : 2 * width, :].T.astype(bf16)


def attend(rows, counts_t, op_embed, cotangent, w_query, w_key, w_value, extra=0):
    slots, blk, width = rows.shape
    ops_count = op_embed.shape[0]
    return pl.pallas_call(
        attend_kernel,
        in_specs=[VMEM_SPEC] * 7,
        out_specs=[VMEM_SPEC] * 3,
        out_shape=[
            jax.ShapeDtypeStruct((slots, blk + extra, width), bf16),
            jax.ShapeDtypeStruct((ops_count, width), bf16),
            jax.ShapeDtypeStruct((3 * width, width), bf16),
        ],
        scratch_shapes=[
            pltpu.VMEM((HEADS * ops_count, width), bf16),
            pltpu.VMEM((HEADS * ops_count, width), bf16),
            pltpu.VMEM((width, ops_count), f32),
            pltpu.VMEM((2 * width, width), f32),
            pltpu.VMEM((width, ops_count), bf16),
        ],
        compiler_params=pltpu.CompilerParams(vmem_limit_bytes=48 << 20),
        name="attend",
    )(
        rows,
        counts_t,
        op_embed,
        cotangent,
        w_query,
        w_key,
        w_value,
    )


def pick_kernel(ids_ref, blocks_ref, out_ref):
    for g in range(out_ref.shape[0]):
        out_ref[g] = blocks_ref[ids_ref[g, 0, 0]]


def pick_blocks(ids, blocks):
    groups = ids.shape[0]
    return pl.pallas_call(
        pick_kernel,
        in_specs=[SMEM_SPEC, VMEM_SPEC],
        out_specs=VMEM_SPEC,
        out_shape=jax.ShapeDtypeStruct((groups,) + blocks.shape[1:], blocks.dtype),
        compiler_params=pltpu.CompilerParams(vmem_limit_bytes=SMALL),
        name="pick_blocks",
    )(ids, blocks)


def fill_kernel(parts_ref, buffer_ref, out_ref, sum_ref, sems):
    sum_ref[...] = jnp.sum(parts_ref[...].astype(f32), axis=0).astype(bf16)
    groups, rows, width = out_ref.shape
    lead = sum_ref.shape[0]
    copies = [
        pltpu.make_async_copy(
            sum_ref, out_ref.at[g, pl.ds(rows - lead, lead), :], sems.at[g]
        )
        for g in range(groups)
    ]
    for copy in copies:
        copy.start()
    for copy in copies:
        copy.wait()


def fill_tail(parts, buffer):
    groups = buffer.shape[0]
    return pl.pallas_call(
        fill_kernel,
        in_specs=[VMEM_SPEC, pl.BlockSpec(memory_space=pl.ANY)],
        out_specs=pl.BlockSpec(memory_space=pl.ANY),
        out_shape=jax.ShapeDtypeStruct(buffer.shape, buffer.dtype),
        scratch_shapes=[
            pltpu.VMEM(parts.shape[1:], bf16),
            pltpu.SemaphoreType.DMA((groups,)),
        ],
        input_output_aliases={1: 0},
        compiler_params=pltpu.CompilerParams(vmem_limit_bytes=SMALL),
        name="fill_tail",
    )(parts, buffer)


def collect_kernel(ids_ref, parts_ref, out_ref, acc_ref):
    shards, rows, width = out_ref.shape
    blocks, blk, _ = acc_ref.shape
    share = blocks * blk // shards
    lead = rows - share
    groups = parts_ref.shape[0]
    acc_ref[...] = jnp.zeros_like(acc_ref)
    total = jnp.zeros((lead, width), f32)
    for g in range(groups):
        acc_ref[ids_ref[g, 0, 0]] += parts_ref[g, 0:blk, :].astype(f32)
        total += parts_ref[g, blk : blk + lead, :].astype(f32)
    total = (total * (1.0 / (groups * shards))).astype(bf16)
    for s in range(shards):
        at = s * share
        out_ref[s, 0:share, :] = acc_ref[at // blk, at % blk : at % blk + share, :].astype(
            bf16
        )
        out_ref[s, share:rows, :] = total


def collect_blocks(ids, parts, blocks, shards):
    groups, rows, width = parts.shape
    share = blocks * BLK // shards
    return pl.pallas_call(
        collect_kernel,
        in_specs=[SMEM_SPEC, VMEM_SPEC],
        out_specs=VMEM_SPEC,
        out_shape=jax.ShapeDtypeStruct((shards, share + rows - BLK, width), bf16),
        scratch_shapes=[pltpu.VMEM((blocks, BLK, width), f32)],
        compiler_params=pltpu.CompilerParams(vmem_limit_bytes=SMALL),
        name="collect_blocks",
    )(ids, parts)


def finish_kernel(parts_ref, machine_ref, *grad_refs):
    shards, rows, width = parts_ref.shape
    share = machine_ref.shape[0]
    lead = rows - share
    total = jnp.zeros((share, width), f32)
    for s in range(shards):
        total += parts_ref[s, 0:share, :].astype(f32)
        at = s * lead
        while at < (s + 1) * lead:
            which, row = at // width, at % width
            size = min((s + 1) * lead - at, width - row)
            start = share + at - s * lead
            grad_refs[which][row : row + size, :] = parts_ref[
                s, start : start + size, :
            ].astype(f32)
            at += size
    machine_ref[...] = total


def finish(parts, share):
    width = parts.shape[2]
    square = jax.ShapeDtypeStruct((width, width), f32)
    return pl.pallas_call(
        finish_kernel,
        in_specs=[VMEM_SPEC],
        out_specs=[VMEM_SPEC] * 4,
        out_shape=[jax.ShapeDtypeStruct((share, width), f32), square, square, square],
        compiler_params=pltpu.CompilerParams(vmem_limit_bytes=SMALL),
        name="finish",
    )(parts)


def swap(x, axis):
    return lax.all_to_all(x, axis, split_axis=0, concat_axis=0, tiled=True)


def per_device(op_embed, machine_embed, cotangent, w_query, w_key, w_value, slot_local, counts):
    groups = lax.axis_size("grp")
    shards = lax.axis_size("ops")
    width = op_embed.shape[1]
    machine_rows = machine_embed.shape[0]
    blocks_here = machine_rows // BLK
    ids = swap(jnp.broadcast_to(slot_local.reshape(groups, 1, 1), (groups, 1, 128)), "grp")
    outgoing = pick_blocks(ids, machine_embed.reshape(blocks_here, BLK, width))
    rows = swap(outgoing, "grp")
    lead = 3 * width // shards
    back, op_grad, wgrad = attend(
        rows, counts.T, op_embed, cotangent, w_query, w_key, w_value, extra=lead
    )
    scattered = swap(wgrad.reshape(shards, lead, width), "ops")
    returned = swap(fill_tail(scattered, back), "grp")
    shares = swap(collect_blocks(ids, returned, blocks_here, shards), "ops")
    machine_grad, grad_wq, grad_wk, grad_wv = finish(shares, machine_rows // shards)
    return (op_grad, machine_grad, grad_wq, grad_wk, grad_wv)


def solution(mesh):
    return jax.shard_map(
        per_device,
        mesh=mesh,
        in_specs=(
            P(("grp", "ops"), None),
            P("grp", None),
            P(("grp", "ops"), None),
            P(),
            P(),
            P(),
            P(("grp", "ops"), None),
            P(("grp", "ops"), None),
        ),
        out_specs=(P(("grp", "ops"), None), P(("grp", "ops"), None), P(), P(), P()),
        check_vma=False,
    )
```
